32 devices in a mesh: ctx: 8 (over y, x, core), tp: 4 (over z).
Axes of the slice: x: 2, y: 2, z: 4, core: 2. Of those that a mesh axis runs over, the one named last changes fastest.
Arguments:
- query_mr: bfloat16 [2048, 8192], P('ctx', 'tp'), may hold values from -6 to 6
- key_mr: bfloat16 [2048, 8192], P('ctx', 'tp'), may hold values from -6 to 6
- value_mr: bfloat16 [2048, 8192], P('ctx', 'tp'), may hold values from -6 to 6
- query_li: bfloat16 [2048, 8192], P('ctx', 'tp'), may hold values from -6 to 6
- key_li: bfloat16 [2048, 8192], P('ctx', 'tp'), may hold values from -6 to 6
- cotangent: bfloat16 [2048, 8192], P('ctx', 'tp'), may hold values from -6 to 6
- mr_taps: float32 [128, 8192], P(None, 'tp'), may hold values from -0.5 to 0.5
- decay_rates: float32 [8], replicated, may hold values from 4.8828126e-05 to 0.03
- residues: float32 [8, 8192], P(None, 'tp'), may hold values from -2 to 2
Outputs:
- grad_query_mr: bfloat16 [2048, 8192], P('ctx', 'tp')
- grad_key_mr: bfloat16 [2048, 8192], P('ctx', 'tp')
- grad_value_mr: bfloat16 [2048, 8192], P('ctx', 'tp')
- grad_query_li: bfloat16 [2048, 8192], P('ctx', 'tp')
- grad_key_li: bfloat16 [2048, 8192], P('ctx', 'tp')
- grad_taps: float32 [128, 8192], P(None, 'tp')
- grad_residues: float32 [8, 8192], P(None, 'tp')
The draws below stay inside these ranges and needn't reach their ends.
All inputs are finite; a program needn't handle non-finite values.
Results may differ from the reference program's by a relative error of at most 0.001.
Values may be sent and summed in bfloat16 or wider, within the bound.
A program may use at most 128 MiB of HBM per device.

```python
import math
import jax
import jax.numpy as jnp
from jax import lax

D = 8192
TAPS = 128
MODES = 8
SEQ = 2048


def levels(key, dims, pieces, least, largest):
    gain = 1.0
    for axis_at, shards_of in pieces:
        draws = jax.random.uniform(jax.random.fold_in(jax.random.fold_in(key, 6), axis_at), (shards_of,), jnp.float32, least / len(pieces), largest / len(pieces))
        gain = gain * jnp.repeat(jnp.exp(draws), dims[axis_at] // shards_of).reshape((-1,) + (1,) * (len(dims) - 1 - axis_at))
    return gain


def gaussian(stream_key, extent, deviation, bound, split=(), held_as=jnp.bfloat16):
    result = jax.random.normal(stream_key, extent, jnp.float32) * deviation
    if len(split) > 0:
        result = levels(stream_key, extent, split, -0.22, 0.18) * result
    return jnp.clip(result, min=-bound, max=bound).astype(held_as)


def setup_inputs(seed: int = 0) -> dict:
    splits = jax.random.split(jax.random.key(seed), 10)
    query_mr = gaussian(splits[0], (SEQ, D), 1.0, 6.0, ((0, 8), (1, 4)))
    key_mr = gaussian(splits[1], (SEQ, D), 1.0, 6.0, ((0, 8), (1, 4)))
    value_mr = gaussian(splits[2], (SEQ, D), 1.0, 6.0, ((0, 8), (1, 4)))
    query_li = gaussian(splits[3], (SEQ, D), 1.0, 6.0, ((0, 8), (1, 4)))
    key_li = gaussian(splits[4], (SEQ, D), 1.0, 6.0, ((0, 8), (1, 4)))
    cotangent = gaussian(splits[5], (SEQ, D), 1.0, 6.0, ((0, 8), (1, 4)))
    mr_taps = gaussian(splits[6], (TAPS, D), TAPS ** -0.5, 0.5, ((1, 4),), jnp.float32)
    decay_rates = jnp.clip(jnp.exp(jax.random.uniform(splits[7], (MODES,), jnp.float32, math.log(4.882812572759576e-05), math.log(0.03))), 4.882812572759576e-05, 0.03)
    residues = gaussian(splits[8], (MODES, D), MODES ** -0.5, 2.0, ((1, 4),), jnp.float32)
    return {"query_mr": query_mr, "key_mr": key_mr, "value_mr": value_mr, "query_li": query_li, "key_li": key_li, "cotangent": cotangent, "mr_taps": mr_taps, "decay_rates": decay_rates, "residues": residues}


highest = lax.Precision.HIGHEST

def causal(signal, kernel, length):
    total = 2 * length
    spectrum = jnp.fft.rfft(signal, total, axis=0) * jnp.fft.rfft(kernel, total, axis=0)
    return jnp.fft.irfft(spectrum, total, axis=0)[:length]

def later_sum(signal, kernel, length):
    return causal(signal[::-1], kernel, length)[::-1]

def lagged(first, second, length):
    return causal(first, second[::-1], length)[::-1]

def reference(query_mr, key_mr, value_mr, query_li, key_li, cotangent, mr_taps, decay_rates, residues):
    length = SEQ
    group_cols = math.gcd(D, 256)
    places = jnp.arange(length, dtype=jnp.float32)
    decay_table = jnp.sqrt(-jnp.expm1(-2.0 * decay_rates))[None, :] * jnp.exp(-places[:, None] * decay_rates[None, :])

    def one_group(index):
        start = index * group_cols

        def columns(array):
            return lax.dynamic_slice_in_dim(array, start, group_cols, 1).astype(jnp.float32)
        taps_block = jnp.concatenate([columns(mr_taps), jnp.zeros((length - TAPS, group_cols), jnp.float32)], 0)
        long_filter = jnp.dot(decay_table, columns(residues), precision=highest)
        key_first = columns(key_mr)
        value_first = columns(value_mr)
        mixed_in = key_first * value_first
        mr_conv = causal(mixed_in, taps_block, length)
        mr_out = columns(query_mr) * mr_conv
        key_second = columns(key_li)
        cotan = columns(cotangent)
        li_input = key_second * mr_out
        li_cotan = cotan * columns(query_li)
        li_conv = causal(li_input, long_filter, length)
        li_back = later_sum(li_cotan, long_filter, length)
        residue_sum = jnp.dot(decay_table.T, lagged(li_input, li_cotan, length), precision=highest)
        grad_query_li = (cotan * li_conv).astype(jnp.bfloat16)
        grad_key_li = (mr_out * li_back).astype(jnp.bfloat16)
        mr_grad = cotan + key_second * li_back
        grad_query_mr = (mr_grad * mr_conv).astype(jnp.bfloat16)
        mr_cotan = mr_grad * columns(query_mr)
        mixed_grad = later_sum(mr_cotan, taps_block, length)
        grad_key_mr = (mixed_grad * value_first).astype(jnp.bfloat16)
        grad_value_mr = (mixed_grad * key_first).astype(jnp.bfloat16)
        tap_sum = lagged(mixed_in, mr_cotan, length)[:TAPS]
        return (grad_query_mr, grad_key_mr, grad_value_mr, grad_query_li, grad_key_li, tap_sum, residue_sum)
    results = lax.map(one_group, jnp.arange(D // group_cols, dtype=jnp.int32))

    def joined(array):
        return jnp.moveaxis(array, 0, 1).reshape(array.shape[1], D)
    factor = 1.0 / math.sqrt(length)
    return (joined(results[0]), joined(results[1]), joined(results[2]), joined(results[3]), joined(results[4]), joined(results[5]) * factor, joined(results[6]) * factor)
```

```python
import math

import numpy as np
import jax
import jax.numpy as jnp
from jax import lax
from jax.sharding import PartitionSpec as P

high = lax.Precision.HIGH


def shifted(value, axis, by):
    size = lax.axis_size(axis)
    pairs = [(i, i + by) for i in range(size) if 0 <= i + by < size]
    return lax.ppermute(value, axis, pairs)


def dft_tables(size, spots):
    angle = (2.0 * np.pi / size) * (np.arange(size // 2)[:, None] + 0.5) * np.asarray(spots)[None, :]
    return np.concatenate([np.cos(angle), -np.sin(angle)], 0)


def mat(table, value):
    return jnp.dot(table, value, precision=high, preferred_element_type=jnp.float32)


def cmul(a, b):
    n = a.shape[0] // 2
    ar, ai, br, bi = a[:n], a[n:], b[:n], b[n:]
    return jnp.concatenate([ar * br - ai * bi, ar * bi + ai * br], 0)


def cmul_conj(a, b):
    n = a.shape[0] // 2
    ar, ai, br, bi = a[:n], a[n:], b[:n], b[n:]
    return jnp.concatenate([ar * br + ai * bi, ar * bi - ai * br], 0)


def carried(state, step_rates, axis, sign):
    size = lax.axis_size(axis)
    total = shifted(state, axis, sign)
    by = 1
    while by < size:
        total = total + jnp.exp(-step_rates * by)[:, None] * shifted(total, axis, sign * by)
        by *= 2
    return total


def per_device(
    query_mr, key_mr, value_mr, query_li, key_li, cotangent, mr_taps, decay_rates, residues
):
    length, channels = query_mr.shape
    taps_len = mr_taps.shape[0]
    seq_len = length * lax.axis_size("ctx")
    f32 = jnp.float32
    size_mr = length + taps_len
    size_li = 2 * length
    ahead_mr = jnp.asarray(dft_tables(size_mr, np.arange(size_mr)), f32)
    back_mr = jnp.asarray((2.0 / size_mr) * dft_tables(size_mr, np.arange(size_mr)).T, f32)
    back_taps = jnp.asarray(
        (2.0 / size_mr) * dft_tables(size_mr, taps_len - np.arange(taps_len)).T, f32
    )
    ahead_li = jnp.asarray(dft_tables(size_li, np.arange(length)), f32)
    back_li = jnp.asarray((2.0 / size_li) * dft_tables(size_li, np.arange(length)).T, f32)

    prior_key, prior_value = shifted(
        (key_mr[length - taps_len :], value_mr[length - taps_len :]), "ctx", 1
    )
    cotan = cotangent.astype(f32)
    li_cotan = cotan * query_li.astype(f32)
    places = jnp.arange(length, dtype=f32)
    rates = decay_rates
    mode_scale = jnp.sqrt(-jnp.expm1(-2.0 * rates))
    rising = jnp.exp(-rates[:, None] * places[None, :])
    falling = jnp.exp(-rates[:, None] * (length - 1.0 - places)[None, :])
    scaled = mode_scale[:, None] * rising
    lead = (mode_scale[:, None] * jnp.exp(-rates[:, None] * (places + 1.0)[None, :])).T
    tail = (mode_scale[:, None] * jnp.exp(-rates[:, None] * (length - places)[None, :])).T
    back_state = mat(rising, li_cotan)
    back_in = carried(back_state, rates * length, "ctx", -1)

    mode_spec = mat(ahead_li, scaled.T)
    filter_spec = mat(mode_spec, residues)
    cotan_spec = mat(ahead_li, li_cotan)
    li_back = mat(back_li, cmul_conj(filter_spec, cotan_spec)) + mat(tail, residues * back_in)

    key_second = key_li.astype(f32)
    query_first = query_mr.astype(f32)
    mr_grad = cotan + key_second * li_back
    mr_cotan = mr_grad * query_first
    next_rows = shifted(mr_cotan[:taps_len], "ctx", -1)

    mixed_in = key_mr.astype(f32) * value_mr.astype(f32)
    mixed_prior = prior_key.astype(f32) * prior_value.astype(f32)
    taps_spec = mat(ahead_mr[:, :taps_len], mr_taps)
    mixed_spec = mat(ahead_mr, jnp.concatenate([mixed_prior, mixed_in], 0))
    mr_conv = mat(back_mr[taps_len:], cmul(taps_spec, mixed_spec))
    mr_out = query_first * mr_conv
    li_input = key_second * mr_out
    front_state = mat(falling, li_input)
    front_in = carried(front_state, rates * length, "ctx", 1)
    input_spec = mat(ahead_li, li_input)
    li_conv = mat(back_li, cmul(filter_spec, input_spec)) + mat(lead, residues * front_in)
    lag_spec = cmul_conj(input_spec, cotan_spec)
    residue_part = (2.0 / size_li) * mat(mode_spec.T, lag_spec) + (
        mode_scale * jnp.exp(-rates)
    )[:, None] * front_state * back_in

    grad_spec = mat(ahead_mr[:, :length], mr_cotan)
    tap_part = mat(back_taps, cmul_conj(grad_spec, mixed_spec))
    factor = 1.0 / math.sqrt(seq_len)
    tap_sum, residue_sum = lax.psum((tap_part * factor, residue_part * factor), "ctx")
    next_spec = mat(ahead_mr[:, length:], next_rows)
    mixed_grad = mat(back_mr[:length], cmul_conj(taps_spec, grad_spec + next_spec))

    bf16 = jnp.bfloat16
    return (
        (mr_grad * mr_conv).astype(bf16),
        (mixed_grad * value_mr.astype(f32)).astype(bf16),
        (mixed_grad * key_mr.astype(f32)).astype(bf16),
        (cotan * li_conv).astype(bf16),
        (mr_out * li_back).astype(bf16),
        tap_sum,
        residue_sum,
    )


def solution(mesh):
    split, cols = P("ctx", "tp"), P(None, "tp")
    return jax.shard_map(
        per_device,
        mesh=mesh,
        in_specs=(split,) * 6 + (cols, P(), cols),
        out_specs=(split,) * 5 + (cols, cols),
        check_vma=False,
    )
```

```python
import math

import numpy as np
import jax
import jax.numpy as jnp
from jax import lax
from jax.experimental import pallas as pl
from jax.experimental.pallas import tpu as pltpu
from jax.sharding import PartitionSpec as P

high = lax.Precision.HIGH


def shifted(value, axis, by):
    size = lax.axis_size(axis)
    pairs = [(i, i + by) for i in range(size) if 0 <= i + by < size]
    return lax.ppermute(value, axis, pairs)


def dft_tables(size, spots):
    angle = (2.0 * np.pi / size) * (np.arange(size // 2)[:, None] + 0.5) * np.asarray(spots)[None, :]
    return np.concatenate([np.cos(angle), -np.sin(angle)], 0)


def mat(table, value):
    return jnp.dot(table, value, precision=high, preferred_element_type=jnp.float32)


def mat_back(table, value):
    return lax.dot_general(
        table,
        value,
        (((0,), (0,)), ((), ())),
        precision=high,
        preferred_element_type=jnp.float32,
    )


def cmul(a, b):
    n = a.shape[0] // 2
    ar, ai, br, bi = a[:n], a[n:], b[:n], b[n:]
    return jnp.concatenate([ar * br - ai * bi, ar * bi + ai * br], 0)


def cmul_conj(a, b):
    n = a.shape[0] // 2
    ar, ai, br, bi = a[:n], a[n:], b[:n], b[n:]
    return jnp.concatenate([ar * br + ai * bi, ar * bi - ai * br], 0)


def greet_all(me, size):
    barrier = pltpu.get_barrier_semaphore()
    for k in range(1, size):
        pl.semaphore_signal(
            barrier,
            inc=1,
            device_id={"ctx": lax.rem(me + k, size)},
            device_id_type=pl.DeviceIdType.MESH,
        )
    pl.semaphore_wait(barrier, size - 1)


def remote(src, dst, send, recv, target):
    return pltpu.make_async_remote_copy(
        src_ref=src,
        dst_ref=dst,
        send_sem=send,
        recv_sem=recv,
        device_id={"ctx": target},
        device_id_type=pl.DeviceIdType.MESH,
    )


def send_states(me, size, sign, state, slots, send, recv):
    for k in range(1, size):
        target = me + sign * k

        @pl.when((target >= 0) & (target < size))
        def _():
            remote(state, slots.at[k - 1], send.at[k - 1], recv.at[k - 1], target).start()


def take_states(me, size, sign, state, slots, send, recv, pows, out):
    out[...] = jnp.zeros_like(out)
    for k in range(1, size):
        source = me - sign * k

        @pl.when((source >= 0) & (source < size))
        def _():
            remote(state, slots.at[k - 1], send.at[k - 1], recv.at[k - 1], source).wait_recv()
            out[...] += pows[:, k - 1 : k] * slots[k - 1]

    for k in range(1, size):
        target = me + sign * k

        @pl.when((target >= 0) & (target < size))
        def _():
            remote(state, slots.at[k - 1], send.at[k - 1], recv.at[k - 1], target).wait_send()


def scan_kernel(size, sign, state, pows, out, slots, send, recv):
    me = lax.axis_index("ctx")
    greet_all(me, size)
    send_states(me, size, sign, state, slots, send, recv)
    take_states(me, size, sign, state, slots, send, recv, pows, out)


def flip(me, bit):
    part = lax.rem(me // (1 << bit), 2)
    return part, me + (1 - 2 * part) * (1 << bit)


def sum_kernel(size, x, state, pows, out, front, acc, got, slots, send, recv, s_send, s_recv):
    me = lax.axis_index("ctx")
    steps = size.bit_length() - 1
    half = x.shape[0] // 2
    greet_all(me, size)
    send_states(me, size, 1, state, slots, s_send, s_recv)
    first = list(range(steps))
    second = first[:1] + first[:0:-1]
    orders = (first, second)
    lows = [0, half]
    offs = [0, half]
    started = []
    for step in range(steps):
        width = half >> (step + 1)
        source = x if step == 0 else acc
        copies = []
        for h in range(2):
            part, partner = flip(me, orders[h][step])
            at = 2 * step + h
            copy = remote(
                source.at[pl.ds(lows[h] + (1 - part) * width, width)],
                got.at[pl.ds(offs[h], width)],
                send.at[at],
                recv.at[at],
                partner,
            )
            copy.start()
            copies.append(copy)
            lows[h] = lows[h] + part * width
        for h in range(2):
            copies[h].wait_recv()
            kept = pl.ds(lows[h], width)
            total = source[kept] + got[pl.ds(offs[h], width)]
            if step == steps - 1:
                out[kept] = total
            else:
                acc[kept] = total
            offs[h] += width
        started += copies
    for step in reversed(range(steps)):
        width = half >> (step + 1)
        copies = []
        for h in range(2):
            part, partner = flip(me, orders[h][step])
            at = 2 * (steps + step) + h
            kept = pl.ds(lows[h], width)
            copy = remote(out.at[kept], out.at[kept], send.at[at], recv.at[at], partner)
            copy.start()
            copies.append(copy)
            lows[h] = lows[h] - part * width
        for copy in copies:
            copy.wait_recv()
        started += copies
    take_states(me, size, 1, state, slots, s_send, s_recv, pows, front)
    for copy in started:
        copy.wait_send()


def in_vmem(count):
    return [pl.BlockSpec(memory_space=pltpu.VMEM)] * count


def device_pows(rates, size):
    far = jnp.exp(-rates[:, None] * jnp.arange(size - 1, dtype=jnp.float32)[None, :])
    return jnp.pad(far, ((0, 0), (0, -(size - 1) % 128)))


def scan_states(state, rates):
    size = lax.axis_size("ctx")
    return pl.pallas_call(
        lambda *refs: scan_kernel(size, -1, *refs),
        out_shape=jax.ShapeDtypeStruct(state.shape, jnp.float32),
        in_specs=in_vmem(2),
        out_specs=pl.BlockSpec(memory_space=pltpu.VMEM),
        scratch_shapes=[
            pltpu.VMEM((size - 1,) + state.shape, jnp.float32),
            pltpu.SemaphoreType.DMA((size - 1,)),
            pltpu.SemaphoreType.DMA((size - 1,)),
        ],
        compiler_params=pltpu.CompilerParams(collective_id=0, has_side_effects=True),
        name="scan_states",
    )(state, device_pows(rates, size))


def summed(parts, state, rates):
    size = lax.axis_size("ctx")
    steps = size.bit_length() - 1
    rows, channels = parts.shape
    tiles = parts.reshape(rows // 8, 8, channels // 128, 128).transpose(0, 2, 1, 3)
    count = rows // 8 * (channels // 128)
    tiles = tiles.reshape(count, 8, 128)
    extra = -count % (2 * size)
    if extra:
        tiles = jnp.pad(tiles, ((0, extra), (0, 0), (0, 0)))
    total, front = pl.pallas_call(
        lambda *refs: sum_kernel(size, *refs),
        out_shape=(
            jax.ShapeDtypeStruct(tiles.shape, jnp.float32),
            jax.ShapeDtypeStruct(state.shape, jnp.float32),
        ),
        in_specs=in_vmem(3),
        out_specs=tuple(in_vmem(2)),
        scratch_shapes=[
            pltpu.VMEM(tiles.shape, jnp.float32),
            pltpu.VMEM(tiles.shape, jnp.float32),
            pltpu.VMEM((size - 1,) + state.shape, jnp.float32),
            pltpu.SemaphoreType.DMA((4 * steps,)),
            pltpu.SemaphoreType.DMA((4 * steps,)),
            pltpu.SemaphoreType.DMA((size - 1,)),
            pltpu.SemaphoreType.DMA((size - 1,)),
        ],
        compiler_params=pltpu.CompilerParams(collective_id=1, has_side_effects=True),
        name="sum_parts",
    )(tiles, state, device_pows(rates, size))
    total = total[:count].reshape(rows // 8, channels // 128, 8, 128).transpose(0, 2, 1, 3)
    return total.reshape(rows, channels), front


def per_device(
    query_mr, key_mr, value_mr, query_li, key_li, cotangent, mr_taps, decay_rates, residues
):
    length, channels = query_mr.shape
    taps_len = mr_taps.shape[0]
    seq_len = length * lax.axis_size("ctx")
    f32 = jnp.float32
    size_mr = length + taps_len
    size_li = 2 * length
    first_mr = jnp.asarray(dft_tables(size_mr, np.arange(length)), f32)
    after_mr = jnp.asarray(dft_tables(size_mr, np.arange(length, size_mr)), f32)
    taps_mr = jnp.asarray(dft_tables(size_mr, np.arange(taps_len)), f32)
    table_li = jnp.asarray(dft_tables(size_li, np.arange(length)), f32)

    mixed_in = key_mr.astype(f32) * value_mr.astype(f32)
    mixed_prior = shifted(mixed_in[length - taps_len :], "ctx", 1)
    cotan = cotangent.astype(f32)
    li_cotan = cotan * query_li.astype(f32)
    places = jnp.arange(length, dtype=f32)
    rates = decay_rates
    mode_scale = jnp.sqrt(-jnp.expm1(-2.0 * rates))
    rising = jnp.exp(-rates[:, None] * places[None, :])
    falling = jnp.exp(-rates[:, None] * (length - 1.0 - places)[None, :])
    scaled = mode_scale[:, None] * rising
    lead = (mode_scale[:, None] * jnp.exp(-rates[:, None] * (places + 1.0)[None, :])).T
    tail = (mode_scale[:, None] * jnp.exp(-rates[:, None] * (length - places)[None, :])).T
    back_state = mat(rising, li_cotan)
    back_in = scan_states(back_state, rates * length)

    mode_spec = (2.0 / size_li) * mat(table_li, scaled.T)
    filter_spec = mat(mode_spec, residues)
    cotan_spec = mat(table_li, li_cotan)
    li_back = mat_back(table_li, cmul_conj(filter_spec, cotan_spec)) + mat(tail, residues * back_in)

    key_second = key_li.astype(f32)
    query_first = query_mr.astype(f32)
    mr_grad = cotan + key_second * li_back
    mr_cotan = mr_grad * query_first
    next_rows = shifted(mr_cotan[:taps_len], "ctx", -1)

    taps_spec = (2.0 / size_mr) * mat(taps_mr, mr_taps)
    mixed_spec = mat(first_mr, mixed_in) - mat(after_mr, mixed_prior)
    mr_conv = mat_back(first_mr, cmul(taps_spec, mixed_spec))
    mr_out = query_first * mr_conv
    li_input = key_second * mr_out
    front_state = mat(falling, li_input)
    input_spec = mat(table_li, li_input)
    lag_spec = cmul_conj(input_spec, cotan_spec)
    residue_part = mat_back(mode_spec, lag_spec) + (
        mode_scale * jnp.exp(-rates)
    )[:, None] * front_state * back_in

    grad_spec = mat(first_mr, mr_cotan)
    tap_part = (2.0 / size_mr) * mat_back(taps_mr, cmul_conj(mixed_spec, grad_spec))
    factor = 1.0 / math.sqrt(seq_len)
    sums, front_in = summed(
        jnp.concatenate([tap_part, residue_part], 0) * factor, front_state, rates * length
    )
    tap_sum, residue_sum = sums[:taps_len], sums[taps_len:]
    li_conv = mat_back(table_li, cmul(filter_spec, input_spec)) + mat(lead, residues * front_in)
    next_spec = mat(after_mr, next_rows)
    mixed_grad = mat_back(first_mr, cmul_conj(taps_spec, grad_spec + next_spec))

    bf16 = jnp.bfloat16
    return (
        (mr_grad * mr_conv).astype(bf16),
        (mixed_grad * value_mr.astype(f32)).astype(bf16),
        (mixed_grad * key_mr.astype(f32)).astype(bf16),
        (cotan * li_conv).astype(bf16),
        (mr_out * li_back).astype(bf16),
        tap_sum,
        residue_sum,
    )


def solution(mesh):
    split, cols = P("ctx", "tp"), P(None, "tp")
    return jax.shard_map(
        per_device,
        mesh=mesh,
        in_specs=(split,) * 6 + (cols, P(), cols),
        out_specs=(split,) * 5 + (cols, cols),
        check_vma=False,
    )
```

```python
import math

import numpy as np
import jax
import jax.numpy as jnp
from jax import lax
from jax.experimental import pallas as pl
from jax.experimental.layout import Layout, with_layout_constraint
from jax.experimental.pallas import tpu as pltpu
from jax.sharding import PartitionSpec as P

high = lax.Precision.HIGH


def shifted(value, axis, by):
    size = lax.axis_size(axis)
    pairs = [(i, i + by) for i in range(size) if 0 <= i + by < size]
    return lax.ppermute(value, axis, pairs)


def dft_tables(size, spots):
    angle = (2.0 * np.pi / size) * (np.arange(size // 2)[:, None] + 0.5) * np.asarray(spots)[None, :]
    return np.concatenate([np.cos(angle), -np.sin(angle)], 0)


def by_rows(value):
    return with_layout_constraint(value, Layout(major_to_minor=(0, 1)))


def mat(table, value):
    result = jnp.dot(table, by_rows(value), precision=high, preferred_element_type=jnp.float32)
    return by_rows(result)


def mat_back(table, value):
    result = lax.dot_general(
        table,
        by_rows(value),
        (((0,), (0,)), ((), ())),
        precision=high,
        preferred_element_type=jnp.float32,
    )
    return by_rows(result)


def cmul(a, b):
    n = a.shape[0] // 2
    ar, ai, br, bi = a[:n], a[n:], b[:n], b[n:]
    return jnp.concatenate([ar * br - ai * bi, ar * bi + ai * br], 0)


def cmul_conj(a, b):
    n = a.shape[0] // 2
    ar, ai, br, bi = a[:n], a[n:], b[:n], b[n:]
    return jnp.concatenate([ar * br + ai * bi, ar * bi - ai * br], 0)


def greet_all(me, size):
    barrier = pltpu.get_barrier_semaphore()
    for k in range(1, size):
        pl.semaphore_signal(
            barrier,
            inc=1,
            device_id={"ctx": lax.rem(me + k, size)},
            device_id_type=pl.DeviceIdType.MESH,
        )
    pl.semaphore_wait(barrier, size - 1)


def remote(src, dst, send, recv, target):
    return pltpu.make_async_remote_copy(
        src_ref=src,
        dst_ref=dst,
        send_sem=send,
        recv_sem=recv,
        device_id={"ctx": target},
        device_id_type=pl.DeviceIdType.MESH,
    )


def send_states(me, size, sign, state, slots, send, recv):
    for k in range(1, size):
        target = me + sign * k

        @pl.when((target >= 0) & (target < size))
        def _():
            remote(state, slots.at[k - 1], send.at[k - 1], recv.at[k - 1], target).start()


def take_states(me, size, sign, state, slots, send, recv, pows, out):
    out[...] = jnp.zeros_like(out)
    for k in range(1, size):
        source = me - sign * k

        @pl.when((source >= 0) & (source < size))
        def _():
            remote(state, slots.at[k - 1], send.at[k - 1], recv.at[k - 1], source).wait_recv()
            out[...] += pows[:, k - 1 : k] * slots[k - 1]

    for k in range(1, size):
        target = me + sign * k

        @pl.when((target >= 0) & (target < size))
        def _():
            remote(state, slots.at[k - 1], send.at[k - 1], recv.at[k - 1], target).wait_send()


def scan_kernel(size, sign, state, pows, out, slots, send, recv):
    me = lax.axis_index("ctx")
    greet_all(me, size)
    send_states(me, size, sign, state, slots, send, recv)
    take_states(me, size, sign, state, slots, send, recv, pows, out)


def flip(me, bit):
    part = lax.rem(me // (1 << bit), 2)
    return part, me + (1 - 2 * part) * (1 << bit)


def sum_kernel(size, x, state, pows, out, front, acc, got, slots, send, recv, s_send, s_recv):
    me = lax.axis_index("ctx")
    steps = size.bit_length() - 1
    half = x.shape[0] // 2
    greet_all(me, size)
    send_states(me, size, 1, state, slots, s_send, s_recv)
    first = list(range(steps))
    second = first[:1] + first[:0:-1]
    orders = (first, second)
    lows = [0, half]
    offs = [0, half]
    started = []
    for step in range(steps):
        width = half >> (step + 1)
        source = x if step == 0 else acc
        copies = []
        for h in range(2):
            part, partner = flip(me, orders[h][step])
            at = 2 * step + h
            copy = remote(
                source.at[pl.ds(lows[h] + (1 - part) * width, width)],
                got.at[pl.ds(offs[h], width)],
                send.at[at],
                recv.at[at],
                partner,
            )
            copy.start()
            copies.append(copy)
            lows[h] = lows[h] + part * width
        for h in range(2):
            copies[h].wait_recv()
            kept = pl.ds(lows[h], width)
            total = source[kept] + got[pl.ds(offs[h], width)]
            if step == steps - 1:
                out[kept] = total
            else:
                acc[kept] = total
            offs[h] += width
        started += copies
    for step in reversed(range(steps)):
        width = half >> (step + 1)
        copies = []
        for h in range(2):
            part, partner = flip(me, orders[h][step])
            at = 2 * (steps + step) + h
            kept = pl.ds(lows[h], width)
            copy = remote(out.at[kept], out.at[kept], send.at[at], recv.at[at], partner)
            copy.start()
            copies.append(copy)
            lows[h] = lows[h] - part * width
        for copy in copies:
            copy.wait_recv()
        started += copies
    take_states(me, size, 1, state, slots, s_send, s_recv, pows, front)
    for copy in started:
        copy.wait_send()


def in_vmem(count):
    return [pl.BlockSpec(memory_space=pltpu.VMEM)] * count


def device_pows(rates, size):
    far = jnp.exp(-rates[:, None] * jnp.arange(size - 1, dtype=jnp.float32)[None, :])
    return jnp.pad(far, ((0, 0), (0, -(size - 1) % 128)))


def scan_states(state, rates):
    size = lax.axis_size("ctx")
    return pl.pallas_call(
        lambda *refs: scan_kernel(size, -1, *refs),
        out_shape=jax.ShapeDtypeStruct(state.shape, jnp.float32),
        in_specs=in_vmem(2),
        out_specs=pl.BlockSpec(memory_space=pltpu.VMEM),
        scratch_shapes=[
            pltpu.VMEM((size - 1,) + state.shape, jnp.float32),
            pltpu.SemaphoreType.DMA((size - 1,)),
            pltpu.SemaphoreType.DMA((size - 1,)),
        ],
        compiler_params=pltpu.CompilerParams(collective_id=0, has_side_effects=True),
        name="scan_states",
    )(state, device_pows(rates, size))


def summed(parts, state, rates):
    size = lax.axis_size("ctx")
    steps = size.bit_length() - 1
    rows, channels = parts.shape
    tiles = parts.reshape(rows // 8, 8, channels // 128, 128).transpose(0, 2, 1, 3)
    count = rows // 8 * (channels // 128)
    tiles = tiles.reshape(count, 8, 128)
    extra = -count % (2 * size)
    if extra:
        tiles = jnp.pad(tiles, ((0, extra), (0, 0), (0, 0)))
    total, front = pl.pallas_call(
        lambda *refs: sum_kernel(size, *refs),
        out_shape=(
            jax.ShapeDtypeStruct(tiles.shape, jnp.float32),
            jax.ShapeDtypeStruct(state.shape, jnp.float32),
        ),
        in_specs=in_vmem(3),
        out_specs=tuple(in_vmem(2)),
        scratch_shapes=[
            pltpu.VMEM(tiles.shape, jnp.float32),
            pltpu.VMEM(tiles.shape, jnp.float32),
            pltpu.VMEM((size - 1,) + state.shape, jnp.float32),
            pltpu.SemaphoreType.DMA((4 * steps,)),
            pltpu.SemaphoreType.DMA((4 * steps,)),
            pltpu.SemaphoreType.DMA((size - 1,)),
            pltpu.SemaphoreType.DMA((size - 1,)),
        ],
        compiler_params=pltpu.CompilerParams(collective_id=1, has_side_effects=True),
        name="sum_parts",
    )(tiles, state, device_pows(rates, size))
    total = total[:count].reshape(rows // 8, channels // 128, 8, 128).transpose(0, 2, 1, 3)
    return total.reshape(rows, channels), front


def per_device(
    query_mr, key_mr, value_mr, query_li, key_li, cotangent, mr_taps, decay_rates, residues
):
    length, channels = query_mr.shape
    taps_len = mr_taps.shape[0]
    seq_len = length * lax.axis_size("ctx")
    f32 = jnp.float32
    size_mr = length + taps_len
    size_li = 2 * length
    first_mr = jnp.asarray(dft_tables(size_mr, np.arange(length)), f32)
    after_mr = jnp.asarray(dft_tables(size_mr, np.arange(length, size_mr)), f32)
    taps_mr = jnp.asarray(dft_tables(size_mr, np.arange(taps_len)), f32)
    table_li = jnp.asarray(dft_tables(size_li, np.arange(length)), f32)

    mixed_in = key_mr.astype(f32) * value_mr.astype(f32)
    mixed_prior = shifted(mixed_in[length - taps_len :], "ctx", 1)
    cotan = cotangent.astype(f32)
    li_cotan = cotan * query_li.astype(f32)
    places = jnp.arange(length, dtype=f32)
    rates = decay_rates
    mode_scale = jnp.sqrt(-jnp.expm1(-2.0 * rates))
    rising = jnp.exp(-rates[:, None] * places[None, :])
    falling = jnp.exp(-rates[:, None] * (length - 1.0 - places)[None, :])
    scaled = mode_scale[:, None] * rising
    lead = (mode_scale[:, None] * jnp.exp(-rates[:, None] * (places + 1.0)[None, :])).T
    tail = (mode_scale[:, None] * jnp.exp(-rates[:, None] * (length - places)[None, :])).T
    back_state = mat(rising, li_cotan)
    back_in = scan_states(back_state, rates * length)

    mode_spec = (2.0 / size_li) * mat(table_li, scaled.T)
    filter_spec = mat(mode_spec, residues)
    cotan_spec = mat(table_li, li_cotan)
    li_back = mat_back(table_li, cmul_conj(filter_spec, cotan_spec)) + mat(tail, residues * back_in)

    key_second = key_li.astype(f32)
    query_first = query_mr.astype(f32)
    mr_grad = cotan + key_second * li_back
    mr_cotan = mr_grad * query_first
    next_rows = shifted(mr_cotan[:taps_len], "ctx", -1)

    taps_spec = (2.0 / size_mr) * mat(taps_mr, mr_taps)
    mixed_spec = mat(first_mr, mixed_in) - mat(after_mr, mixed_prior)
    mr_conv = mat_back(first_mr, cmul(taps_spec, mixed_spec))
    mr_out = query_first * mr_conv
    li_input = key_second * mr_out
    front_state = mat(falling, li_input)
    input_spec = mat(table_li, li_input)
    lag_spec = cmul_conj(input_spec, cotan_spec)
    residue_part = mat_back(mode_spec, lag_spec) + (
        mode_scale * jnp.exp(-rates)
    )[:, None] * front_state * back_in

    grad_spec = mat(first_mr, mr_cotan)
    tap_part = (2.0 / size_mr) * mat_back(taps_mr, cmul_conj(mixed_spec, grad_spec))
    factor = 1.0 / math.sqrt(seq_len)
    parts = jnp.concatenate([tap_part, residue_part], 0) * factor
    parts, next_rows = lax.optimization_barrier((parts, next_rows))
    sums, front_in = summed(parts, front_state, rates * length)
    tap_sum, residue_sum = sums[:taps_len], sums[taps_len:]
    li_conv = mat_back(table_li, cmul(filter_spec, input_spec)) + mat(lead, residues * front_in)
    next_spec = mat(after_mr, next_rows)
    mixed_grad = mat_back(first_mr, cmul_conj(taps_spec, grad_spec + next_spec))

    bf16 = jnp.bfloat16
    return (
        (mr_grad * mr_conv).astype(bf16),
        (mixed_grad * value_mr.astype(f32)).astype(bf16),
        (mixed_grad * key_mr.astype(f32)).astype(bf16),
        (cotan * li_conv).astype(bf16),
        (mr_out * li_back).astype(bf16),
        tap_sum,
        residue_sum,
    )


def solution(mesh):
    split, cols = P("ctx", "tp"), P(None, "tp")
    return jax.shard_map(
        per_device,
        mesh=mesh,
        in_specs=(split,) * 6 + (cols, P(), cols),
        out_specs=(split,) * 5 + (cols, cols),
        check_vma=False,
    )
```
